32 devices in a mesh: sx: 8 (over z, core), sy: 4 (over y, x).
Axes of the slice: x: 2, y: 2, z: 4, core: 2. Of those that a mesh axis runs over, the one named last changes fastest.
Arguments:
- local_source: float32 [8, 4, 768, 256], P('sx', 'sy'), may hold values from -6 to 6
- schur: bfloat16 [8, 4, 768, 768], P('sx', 'sy')
- local_inverse: bfloat16 [8, 4, 768, 768], P('sx', 'sy')
- primal_basis: bfloat16 [8, 4, 768, 32], P('sx', 'sy'), may hold values from -0.21875 to 0.21875
- coarse_inverse: float32 [8, 4, 32, 32], P('sx', 'sy')
- primal_map: int32 [8, 4, 32], P('sx', 'sy'), may hold values from 0 to 255, as said below
- shared_count: int32 [8, 4, 8], P('sx', 'sy'), may hold values from 0 to 64, as said below
- row_order: int32 [8, 4, 768], P('sx', 'sy'), may hold values from 0 to 767, each once within a row
Outputs:
- solution: float32 [8, 4, 768, 256], P('sx', 'sy')
- residual: float32 [8, 4, 768, 256], P('sx', 'sy')
The draws below stay inside these ranges and needn't reach their ends.
Inputs may be any that keep to these rules, and one draw needn't show every extreme that they name: shared_count[i, j, d] equals shared_count[i + a, j + b, 7 - d] for offset d = (a, b), and is 0 where (i + a, j + b) lies outside the 8 x 4 grid. A neighbour at offset (0, 1), (0, -1), (1, 0) or (-1, 0) inside the grid shares a quarter of 64 rows or more; a diagonal neighbour shares none or a quarter of 64 or more. Some pair shares exactly 64. primal_map[i, j, m] lies in block (i - 1) mod 8, i or (i + 1) mod 8, block b holding the coarse unknowns b * 32 to (b + 1) * 32 - 1. Each subdomain's row_order holds every row once.
All inputs are finite; a program needn't handle non-finite values.
Results may differ from the reference program's by a relative error of at most 0.0072.
Values sent between devices are 32-bit elements; how exact they have to be, the bound alone decides.
A program may use at most 64 MiB of HBM per device.

```python
import math
from functools import partial
import jax
import jax.numpy as jnp
from jax import lax

NI = 768
NPRIM = 32
CB = 32
MROW = 64
P_SIZE = 256
ITERS = 3
N_SX = 8
N_SY = 4


directions = ((-1, -1), (-1, 0), (-1, 1), (0, -1), (0, 1), (1, -1), (1, 0), (1, 1))


def symmetric_noise(key, order, strength):
    raw = jax.random.normal(key, (order, order), jnp.float32)
    return (raw + raw.T) * (strength / math.sqrt(2.0 * order))


def subdomain_pair(key):
    first_key, second_key, third_key = jax.random.split(key, 3)
    scales = jnp.exp(jax.random.uniform(first_key, (NI,), jnp.float32, math.log(0.5), math.log(2.0)))
    coupling = symmetric_noise(second_key, NI, 0.35)
    extra = symmetric_noise(third_key, NI, 0.12)
    root = jnp.sqrt(scales)
    identity = jnp.eye(NI, dtype=jnp.float32)
    schur_block = root[:, None] * (identity + coupling) * root[None, :]
    inverse_block = (identity - coupling + extra) / (root[:, None] * root[None, :])
    return (schur_block, inverse_block)


def draw_schur(key, part):
    keys = jax.random.split(jax.random.fold_in(key, 11), N_SX * N_SY)
    blocks = lax.map(lambda one: subdomain_pair(one)[0], keys)
    return blocks.reshape(N_SX, N_SY, NI, NI).astype(jnp.bfloat16)


def draw_local_inverse(key, part):
    keys = jax.random.split(jax.random.fold_in(key, 11), N_SX * N_SY)
    blocks = lax.map(lambda one: subdomain_pair(one)[1], keys)
    return blocks.reshape(N_SX, N_SY, NI, NI).astype(jnp.bfloat16)


def coarse_block(key):
    first_key, second_key = jax.random.split(key)
    scales = jnp.exp(jax.random.uniform(first_key, (CB,), jnp.float32, math.log(0.5), math.log(2.0)))
    root = jnp.sqrt(scales)
    noise = symmetric_noise(second_key, CB, 0.3)
    return root[:, None] * (jnp.eye(CB, dtype=jnp.float32) + noise) * root[None, :]


def draw_coarse_inverse(key, part):
    keys = jax.random.split(jax.random.fold_in(key, 23), N_SX * N_SY)
    blocks = lax.map(coarse_block, keys)
    return blocks.reshape(N_SX, N_SY, CB, CB).astype(jnp.float32)


def draw_primal_map(key, part):
    first_key, second_key = jax.random.split(jax.random.fold_in(key, 31))
    offset = jax.random.randint(first_key, (N_SX, N_SY, NPRIM), -1, 2)
    within = jax.random.randint(second_key, (N_SX, N_SY, NPRIM), 0, CB)
    first_index = jnp.arange(N_SX, dtype=jnp.int32)[:, None, None]
    block = (first_index + offset + N_SX) % N_SX
    return (block * CB + within).astype(jnp.int32)


def shifted(values, first, second):
    padded = jnp.pad(values, ((1, 1), (1, 1)))
    return padded[1 + first:1 + first + N_SX, 1 + second:1 + second + N_SY]


def draw_shared_count(key, part):
    first_key, second_key, third_key, fourth_key = jax.random.split(jax.random.fold_in(key, 41), 4)
    forward = jax.random.randint(first_key, (N_SX, N_SY, 4), MROW // 4, MROW + 1)
    present = jax.random.randint(second_key, (N_SX, N_SY, 4), 0, 2)
    diagonal = jnp.array([0, 1, 0, 1], dtype=jnp.int32)
    forward = forward * (1 - diagonal + diagonal * present)
    chosen_row = jax.random.randint(third_key, (), 0, N_SX - 1)
    chosen_col = jax.random.randint(fourth_key, (), 0, N_SY)
    row_index = jnp.arange(N_SX, dtype=jnp.int32)[:, None]
    col_index = jnp.arange(N_SY, dtype=jnp.int32)[None, :]
    hit = (row_index == chosen_row) & (col_index == chosen_col)
    forward = forward.at[:, :, 2].set(jnp.where(hit, MROW, forward[:, :, 2]))
    columns = []
    for place in range(4):
        first, second = directions[4 + place]
        inside = (row_index + first >= 0) & (row_index + first < N_SX) & (col_index + second >= 0) & (col_index + second < N_SY)
        columns.append(jnp.where(inside, forward[:, :, place], 0))
    counts = []
    for slot in range(8):
        if slot >= 4:
            counts.append(columns[slot - 4])
        else:
            first, second = directions[slot]
            counts.append(shifted(columns[7 - slot - 4], first, second))
    return jnp.stack(counts, axis=2).astype(jnp.int32)


def steps_of(rng, extent, cuts, low, largest):
    factor_of = 1.0
    for axis_at, blocks in cuts:
        draws = jax.random.uniform(jax.random.fold_in(jax.random.fold_in(rng, 6), axis_at), (blocks,), jnp.float32, low / len(cuts), largest / len(cuts))
        factor_of = factor_of * jnp.repeat(jnp.exp(draws), extent[axis_at] // blocks).reshape((-1,) + (1,) * (len(extent) - 1 - axis_at))
    return factor_of


def centred(rng, dims, scale, most, pieces=(), kind=jnp.bfloat16):
    gain = steps_of(rng, dims, pieces, -0.22, 0.18) if pieces else 1.0
    entries = jax.random.normal(rng, dims, jnp.float32) * scale * gain
    return jnp.minimum(jnp.maximum(entries, -most), most).astype(kind)


def setup_inputs(seed: int = 0) -> dict:
    key_of = jax.random.split(jax.random.key(seed), 9)
    return {
        "local_source": centred(key_of[0], (N_SX, N_SY, NI, P_SIZE), 1.0, 6.0, ((0, 8), (1, 4)), jnp.float32),
        "schur": draw_schur(jax.random.fold_in(key_of[8], 71), 0),
        "local_inverse": draw_local_inverse(jax.random.fold_in(key_of[8], 71), 0),
        "primal_basis": centred(key_of[3], (N_SX, N_SY, NI, NPRIM), NI ** -0.5, 0.21875, ((0, 8), (1, 4))),
        "coarse_inverse": draw_coarse_inverse(jax.random.fold_in(key_of[8], 71), 0),
        "primal_map": draw_primal_map(jax.random.fold_in(key_of[8], 71), 0),
        "shared_count": draw_shared_count(jax.random.fold_in(key_of[8], 71), 0),
        "row_order": jax.vmap(lambda own: jax.random.permutation(own, NI))(jax.random.split(key_of[7], N_SX * N_SY)).reshape((N_SX, N_SY, NI)).astype(jnp.int32),
    }


directions = ((-1, -1), (-1, 0), (-1, 1), (0, -1), (0, 1), (1, -1), (1, 0), (1, 1))
centre = 1.6
spread = 1.4


def group_rows(counts, order, rows):
    offsets = jnp.cumsum(counts) - counts
    column = jnp.arange(rows, dtype=jnp.int32)
    places = jnp.minimum(offsets[:, None] + column[None, :], order.shape[0] - 1).astype(jnp.int32)
    row_map = order[places]
    valid = (column[None, :] < counts[:, None]).astype(jnp.float32)
    return row_map, valid


def neighbour(values, first, second):
    widths = ((1, 1), (1, 1)) + ((0, 0),) * (values.ndim - 2)
    padded = jnp.pad(values, widths)
    return padded[1 + first:1 + first + N_SX, 1 + second:1 + second + N_SY]


def deposit(vector, row_map, incoming):
    return vector.at[row_map.reshape(-1)].add(incoming.reshape(-1, vector.shape[-1]))


def assemble(vector, row_map, valid):
    index = row_map.reshape(N_SX, N_SY, 8 * MROW, 1)
    taken = jnp.take_along_axis(vector, index, axis=2).reshape(N_SX, N_SY, 8, MROW, P_SIZE)
    taken = taken * valid[..., None]
    incoming = jnp.stack([neighbour(taken[:, :, 7 - slot], directions[slot][0], directions[slot][1]) for slot in range(8)], axis=2)
    incoming = incoming * valid[..., None]
    return jax.vmap(jax.vmap(deposit))(vector, row_map, incoming)


def batched(left, right):
    flat_left = left.reshape((-1,) + left.shape[2:])
    flat_right = right.reshape((-1,) + right.shape[2:])
    out = lax.map(lambda pair: jnp.dot(pair[0], pair[1], preferred_element_type=jnp.float32), (flat_left, flat_right))
    return out.reshape(left.shape[:2] + out.shape[1:])


def batched_left_t(left, right):
    flat_left = left.reshape((-1,) + left.shape[2:])
    flat_right = right.reshape((-1,) + right.shape[2:])
    out = lax.map(lambda pair: lax.dot_general(pair[0], pair[1], (((0,), (0,)), ((), ())), preferred_element_type=jnp.float32), (flat_left, flat_right))
    return out.reshape(left.shape[:2] + out.shape[1:])


def reference(local_source, schur, local_inverse, primal_basis, coarse_inverse, primal_map, shared_count, row_order):
    row_map, valid = jax.vmap(jax.vmap(partial(group_rows, rows=MROW)))(shared_count, row_order)
    marks = jax.vmap(jax.vmap(lambda rm, va: jnp.zeros((NI,), jnp.float32).at[rm.reshape(-1)].add(va.reshape(-1))))(row_map, valid)
    weight = (1.0 - 0.5 * marks)[..., None]
    column_ids = jnp.broadcast_to(jnp.arange(N_SY, dtype=jnp.int32)[None, :, None], primal_map.shape)

    def precondition(residual):
        scaled = (weight * residual).astype(jnp.bfloat16)
        local = batched(local_inverse, scaled)
        primal = batched_left_t(primal_basis, scaled)
        coarse_rhs = jnp.zeros((N_SY, N_SX * CB, P_SIZE), jnp.float32).at[column_ids, primal_map].add(primal)
        blocks = coarse_rhs.reshape(N_SY, N_SX, CB, P_SIZE)
        solved = jnp.einsum('ijab,jibp->ijap', coarse_inverse, blocks, precision=lax.Precision.HIGHEST)
        column_sol = jnp.transpose(solved, (1, 0, 2, 3)).reshape(N_SY, N_SX * CB, P_SIZE)
        picked = column_sol[column_ids, primal_map].astype(jnp.bfloat16)
        local = local + batched(primal_basis, picked)
        return assemble(weight * local, row_map, valid)

    right = assemble(local_source, row_map, valid)
    solution = jnp.zeros_like(right)
    residual = right
    sigma = centre / spread
    rho = 1.0 / sigma
    direction = jnp.zeros_like(right)
    for step in range(ITERS):
        update = precondition(residual)
        if step == 0:
            direction = update / centre
            rho = 1.0 / sigma
        else:
            rho_new = 1.0 / (2.0 * sigma - rho)
            direction = (rho_new * rho) * direction + (2.0 * rho_new / spread) * update
            rho = rho_new
        solution = solution + direction
        image = assemble(batched(schur, direction.astype(jnp.bfloat16)), row_map, valid)
        residual = residual - image
    return solution, residual
```

```python
import functools

import jax
import jax.numpy as jnp
from jax import lax
from jax.experimental import pallas as pl
from jax.experimental.pallas import tpu as pltpu
from jax.sharding import PartitionSpec as P

MROW = 64
ITERS = 3
CHUNKS = 4
LANES = 128
MESH = pl.DeviceIdType.MESH

directions = ((-1, -1), (-1, 0), (-1, 1), (0, -1), (0, 1), (1, -1), (1, 0), (1, 1))
send_order = (0, 2, 5, 7, 3, 4, 1, 6)
ring = (-2, -1, 1, 2)
centre = 1.6
spread = 1.4
f32 = jnp.float32
bf16 = jnp.bfloat16
NN = (((1,), (0,)), ((), ()))
TN = (((0,), (0,)), ((), ()))


def mm(left, right, dims=NN):
    return lax.dot_general(left, right, dims, preferred_element_type=f32)


def exact(left, right, dims=NN):
    return lax.dot_general(left, right, dims, precision=lax.Precision.HIGHEST, preferred_element_type=f32)


def split(value):
    high = value.astype(bf16)
    return high, (value - high.astype(f32)).astype(bf16)


def select_rows(value, one_hot):
    count = value.shape[0]
    both = mm(jnp.concatenate(split(value), axis=0), one_hot)
    return both[:count] + both[count:]


def iota(shape, axis):
    return lax.broadcasted_iota(jnp.int32, shape, axis)


def kernel(
    nx, ny,
    source, schur, inverse, basis, coarse, pmap, counts, order,
    sol_out, res_out,
    source_v, inverse_v, schur_v, gather, scatter, inverse_g, inverse_w, schur_g, schur_w, basis_q, picked_g, picked_w,
    cmat, weight, res, sol, direction, local, shared, out_buf, in_buf, prim_buf, maps, coarses,
    load_sem, out_send, out_recv, prim_send, prim_recv, meta_send, meta_recv,
):
    me_x, me_y = lax.axis_index("sx"), lax.axis_index("sy")
    rows, width = source.shape[2], source.shape[3]
    block = coarse.shape[2]
    modes = basis.shape[2]
    slots = 8 * MROW
    links = len(ring)
    stages = 1 + 2 * ITERS
    wide = width // CHUNKS
    half = wide // 2
    parts = LANES // modes
    quarter = wide // parts

    def inside(d):
        a, b = directions[d]
        x, y = me_x + a, me_y + b
        return (x >= 0) & (x < nx) & (y >= 0) & (y < ny)

    def peer(d):
        a, b = directions[d]
        return (me_x + a, me_y + b)

    def ring_peer(s):
        return (lax.rem(me_x + s + nx, nx), me_y)

    load_source = pltpu.make_async_copy(source.at[0, 0], source_v, load_sem.at[0])
    load_inverse = pltpu.make_async_copy(inverse.at[0, 0], inverse_v, load_sem.at[1])
    load_schur = pltpu.make_async_copy(schur.at[0, 0], schur_v, load_sem.at[2])
    load_source.start()
    load_inverse.start()
    load_schur.start()

    barrier = pltpu.get_barrier_semaphore()
    total = jnp.int32(links)
    for d in range(8):
        total = total + inside(d).astype(jnp.int32)

        @pl.when(inside(d))
        def _(d=d):
            pl.semaphore_signal(barrier, inc=1, device_id=peer(d), device_id_type=MESH)

    for s in ring:
        pl.semaphore_signal(barrier, inc=1, device_id=ring_peer(s), device_id_type=MESH)

    slot = iota((1, slots), 1)
    begins = jnp.zeros((1, slots), jnp.int32)
    sizes = jnp.zeros((1, slots), jnp.int32)
    start = jnp.int32(0)
    for d in range(8):
        count = counts[0, 0, d]
        mine = slot // MROW == d
        begins = jnp.where(mine, start, begins)
        sizes = jnp.where(mine, count, sizes)
        start = start + count
    place = lax.rem(slot, MROW)
    position = jnp.where(place < sizes, begins + place, -1)
    row_of = iota((rows, slots), 0)
    scatter[...] = jnp.where(row_of == position, 1.0, 0.0).astype(bf16)
    digit = iota((16, rows), 0)
    ids = order[0]
    digits = jnp.where(digit == 0, ids // 256, jnp.where(digit == 1, lax.rem(ids, 256), 1))
    found = mm(digits.astype(f32).astype(bf16), scatter[...])
    target = jnp.where(found[2:3] > 0.5, 256.0 * found[0:1] + found[1:2], -1.0)
    scatter[...] = jnp.where(row_of == target.astype(jnp.int32), 1.0, 0.0).astype(bf16)

    low_lanes = iota((half, LANES), 1) < MROW

    def out_copy(stage, c, d):
        return pltpu.make_async_remote_copy(
            src_ref=out_buf.at[d, stage, c],
            dst_ref=in_buf.at[7 - d, stage, c],
            send_sem=out_send.at[d],
            recv_sem=out_recv.at[stage, c, 7 - d],
            device_id=peer(d),
            device_id_type=MESH,
        )

    def in_copy(stage, c, d):
        return pltpu.make_async_remote_copy(
            src_ref=out_buf.at[7 - d, stage, c],
            dst_ref=in_buf.at[d, stage, c],
            send_sem=out_send.at[7 - d],
            recv_sem=out_recv.at[stage, c, d],
            device_id=peer(d),
            device_id_type=MESH,
        )

    def pack(stage, c, value):
        for t in range(slots // LANES):
            tile = value[:, t * LANES:(t + 1) * LANES]
            top, low = tile[:half], tile[half:]
            out_buf[2 * t, stage, c] = jnp.where(low_lanes, top, pltpu.roll(low, MROW, 1))
            out_buf[2 * t + 1, stage, c] = jnp.where(low_lanes, pltpu.roll(top, MROW, 1), low)

    def send_all(stage, c):
        for d in send_order:
            @pl.when(inside(d))
            def _(d=d):
                out_copy(stage, c, d).start()

    def receive(stage, c):
        for d in range(8):
            @pl.when(inside(d))
            def _(d=d):
                in_copy(stage, c, d).wait_recv()
        tops, lows = [], []
        for t in range(slots // LANES):
            first, second = in_buf[2 * t, stage, c], in_buf[2 * t + 1, stage, c]
            tops.append(jnp.where(low_lanes, first, pltpu.roll(second, MROW, 1)))
            lows.append(jnp.where(low_lanes, pltpu.roll(first, MROW, 1), second))
        value = jnp.concatenate([jnp.concatenate(tops, axis=1), jnp.concatenate(lows, axis=1)], axis=0)
        return select_rows(value, gather[...])

    def ring_copies(src, dst, send, recv):
        return [
            pltpu.make_async_remote_copy(
                src_ref=src, dst_ref=dst(links - 1 - at), send_sem=send(at), recv_sem=recv(links - 1 - at),
                device_id=ring_peer(s), device_id_type=MESH,
            )
            for at, s in enumerate(ring)
        ]

    def prim_copies(step, c):
        return ring_copies(
            prim_buf.at[links, step, c], lambda t: prim_buf.at[t, step, c],
            lambda t: prim_send.at[t], lambda t: prim_recv.at[step, c, t],
        )

    def chunk(c):
        return slice(c * wide, (c + 1) * wide)

    for d in range(8):
        @pl.when(jnp.logical_not(inside(d)))
        def _(d=d):
            in_buf[d] = jnp.zeros(in_buf.shape[1:], f32)

    load_source.wait()
    for at in range(width // LANES):
        res[at * LANES:(at + 1) * LANES, :] = source_v[:, at * LANES:(at + 1) * LANES].T
    for c in range(CHUNKS):
        pack(0, c, select_rows(res[chunk(c), :], scatter[...]))
        if c == 0:
            pl.semaphore_wait(barrier, total)
        send_all(0, c)

    map_copies = ring_copies(
        pmap.at[0, 0], lambda t: maps.at[t], lambda t: meta_send.at[0, t], lambda t: meta_recv.at[0, t]
    )
    coarse_copies = ring_copies(
        coarse.at[0, 0], lambda t: coarses.at[t], lambda t: meta_send.at[1, t], lambda t: meta_recv.at[1, t]
    )
    for copy in map_copies + coarse_copies:
        copy.start()

    column = jnp.broadcast_to(target, (8, slots)).T[:, 0:1].astype(jnp.int32)
    gather[...] = jnp.where(iota((slots, rows), 1) == column, 1.0, 0.0).astype(bf16)
    marks = mm(jnp.ones((16, slots), bf16), gather[...])
    weight[...] = 1.0 - 0.5 * marks[:8]
    scale = weight[0:1, :]
    halved = (scatter[...].astype(f32) * 0.5).astype(bf16)
    basis_t = basis[0, 0]
    basis_q[...] = jnp.concatenate([basis_t.astype(f32)] * parts, axis=0).T.astype(bf16)
    picked_g[...] = jnp.concatenate([mm(basis_t, halved)] * parts, axis=0).astype(bf16)
    picked_w[...] = jnp.concatenate([basis_t.astype(f32) * scale] * parts, axis=0).astype(bf16)
    load_inverse.wait()
    inverse_w[...] = inverse_v[...].T
    inverse_g[...] = mm(inverse_w[...], halved).astype(bf16)
    inverse_w[...] = (inverse_w[...].astype(f32) * scale).astype(bf16)
    load_schur.wait()
    schur_w[...] = schur_v[...].T
    schur_g[...] = mm(schur_w[...], scatter[...]).astype(bf16)

    for copy in map_copies + coarse_copies:
        copy.wait_recv()

    slot_iota = iota((3 * block, modes), 0)

    def chooser(ids):
        relative = lax.rem(ids // block - me_x + 1 + 2 * nx, nx)
        place = relative * block + lax.rem(ids, block)
        return jnp.where(slot_iota == place, 1.0, 0.0).astype(f32)

    own = chooser(pmap[0, 0])
    blocks = (coarses[1], coarse[0, 0], coarses[2])
    chosen = jnp.concatenate([chooser(maps[t]) for t in range(links)] + [own], axis=1)
    solved = jnp.concatenate(
        [exact(blocks[t], chosen[t * block:(t + 1) * block, :]) for t in range(3)], axis=0
    )
    mapped = exact(solved, jnp.concatenate([own] * parts, axis=1), TN)
    same = iota((LANES, LANES), 0) // modes == iota((LANES, LANES), 1) // modes
    for t in range(links + 1):
        tiled = jnp.where(same, jnp.concatenate([mapped[t * modes:(t + 1) * modes]] * parts, axis=0), 0.0)
        high, low = split(tiled)
        cmat[t * LANES:(t + 1) * LANES, :LANES] = high
        cmat[t * LANES:(t + 1) * LANES, LANES:] = low

    part_of = iota((quarter, LANES), 1) // modes

    def begin(step, c):
        scaled = (weight[0:1, :] * res[chunk(c), :]).astype(bf16)
        primal = mm(scaled, basis_q[...])
        packed = primal[:quarter]
        for q in range(1, parts):
            packed = jnp.where(part_of == q, primal[q * quarter:(q + 1) * quarter], packed)
        prim_buf[links, step, c] = packed
        for copy in prim_copies(step, c):
            copy.start()
        shared[chunk(c), :] = mm(scaled, inverse_g[...])
        local[chunk(c), :] = mm(scaled, inverse_w[...])

    def finish(step, c):
        for copy in prim_copies(step, c):
            copy.wait_recv()
        primal = jnp.concatenate([prim_buf[t, step, c] for t in range(links + 1)], axis=1)
        both = mm(jnp.concatenate(split(primal), axis=0), cmat[...])
        packed = both[:quarter, :LANES] + (both[quarter:, :LANES] + both[:quarter, LANES:])
        picked = jnp.concatenate(
            [jnp.where(part_of == q, packed, 0.0) for q in range(parts)], axis=0
        ).astype(bf16)
        pack(1 + 2 * step, c, shared[chunk(c), :] + mm(picked, picked_g[...]))
        send_all(1 + 2 * step, c)
        local[chunk(c), :] = local[chunk(c), :] + mm(picked, picked_w[...])

    for c in range(CHUNKS):
        res[chunk(c), :] = res[chunk(c), :] + receive(0, c)
        begin(0, c)

    sigma = centre / spread
    rho = 1.0 / sigma
    for step in range(ITERS):
        stage = 1 + 2 * step
        for c in range(CHUNKS):
            finish(step, c)
        if step > 0:
            rho_new = 1.0 / (2.0 * sigma - rho)
            keep, gain = rho_new * rho, 2.0 * rho_new / spread
            rho = rho_new
        for c in range(CHUNKS):
            update = local[chunk(c), :] + receive(stage, c)
            if step == 0:
                moved = update / centre
                sol[chunk(c), :] = moved
            else:
                moved = keep * direction[chunk(c), :] + gain * update
                sol[chunk(c), :] = sol[chunk(c), :] + moved
            direction[chunk(c), :] = moved
            rounded = moved.astype(bf16)
            pack(stage + 1, c, mm(rounded, schur_g[...]))
            send_all(stage + 1, c)
            local[chunk(c), :] = mm(rounded, schur_w[...])
        if step + 1 == ITERS:
            for at in range(width // LANES):
                sol_out[0, 0, :, at * LANES:(at + 1) * LANES] = sol[at * LANES:(at + 1) * LANES, :].T
        for c in range(CHUNKS):
            res[chunk(c), :] = res[chunk(c), :] - (local[chunk(c), :] + receive(stage + 1, c))
            if step + 1 < ITERS:
                begin(step + 1, c)
    for at in range(width // LANES):
        res_out[0, 0, :, at * LANES:(at + 1) * LANES] = res[at * LANES:(at + 1) * LANES, :].T

    for copy in map_copies + coarse_copies:
        copy.wait_send()
    for at, s in enumerate(ring):
        pltpu.make_async_remote_copy(
            src_ref=prim_buf.at[links], dst_ref=prim_buf.at[links - 1 - at],
            send_sem=prim_send.at[at], recv_sem=prim_recv.at[0, 0, 0],
            device_id=ring_peer(s), device_id_type=MESH,
        ).wait_send()
    for d in range(8):
        @pl.when(inside(d))
        def _(d=d):
            pltpu.make_async_remote_copy(
                src_ref=out_buf.at[d], dst_ref=in_buf.at[7 - d],
                send_sem=out_send.at[d], recv_sem=out_recv.at[0, 0, 0],
                device_id=peer(d), device_id_type=MESH,
            ).wait_send()


def solution(mesh):
    nx, ny = mesh.shape["sx"], mesh.shape["sy"]

    def body(source, schur, inverse, basis, coarse, pmap, counts, order):
        rows, width = source.shape[2:]
        modes, block = basis.shape[3], coarse.shape[2]
        slots, wide, stages, links = 8 * MROW, width // CHUNKS, 1 + 2 * ITERS, len(ring)
        half, quarter = wide // 2, wide * modes // LANES
        vmem = pl.BlockSpec(memory_space=pltpu.VMEM)
        hbm = pl.BlockSpec(memory_space=pl.ANY)
        smem = pl.BlockSpec(memory_space=pltpu.SMEM)
        dma = pltpu.SemaphoreType.DMA
        shape = jax.ShapeDtypeStruct(source.shape, f32)
        return pl.pallas_call(
            functools.partial(kernel, nx, ny),
            out_shape=(shape, shape),
            in_specs=[hbm, hbm, hbm, vmem, vmem, vmem, smem, vmem],
            out_specs=(vmem, vmem),
            scratch_shapes=[
                pltpu.VMEM((rows, width), f32),
                pltpu.VMEM((rows, rows), bf16),
                pltpu.VMEM((rows, rows), bf16),
                pltpu.VMEM((slots, rows), bf16),
                pltpu.VMEM((rows, slots), bf16),
                pltpu.VMEM((rows, slots), bf16),
                pltpu.VMEM((rows, rows), bf16),
                pltpu.VMEM((rows, slots), bf16),
                pltpu.VMEM((rows, rows), bf16),
                pltpu.VMEM((rows, LANES), bf16),
                pltpu.VMEM((LANES, slots), bf16),
                pltpu.VMEM((LANES, rows), bf16),
                pltpu.VMEM(((links + 1) * LANES, 2 * LANES), bf16),
                pltpu.VMEM((8, rows), f32),
                pltpu.VMEM((width, rows), f32),
                pltpu.VMEM((width, rows), f32),
                pltpu.VMEM((width, rows), f32),
                pltpu.VMEM((width, rows), f32),
                pltpu.VMEM((width, slots), f32),
                pltpu.VMEM((8, stages, CHUNKS, half, LANES), f32),
                pltpu.VMEM((8, stages, CHUNKS, half, LANES), f32),
                pltpu.VMEM((links + 1, ITERS, CHUNKS, quarter, LANES), f32),
                pltpu.VMEM((links, 1, modes), jnp.int32),
                pltpu.VMEM((links, block, block), f32),
                dma((3,)),
                dma((8,)),
                dma((stages, CHUNKS, 8)),
                dma((links,)),
                dma((ITERS, CHUNKS, links)),
                dma((2, links)),
                dma((2, links)),
            ],
            compiler_params=pltpu.CompilerParams(
                collective_id=0, has_side_effects=True, vmem_limit_bytes=56 * 1024 * 1024
            ),
        )(source, schur, inverse, jnp.swapaxes(basis, 2, 3), coarse, pmap[:, :, None, :], counts, order)

    placed = (P("sx", "sy", None, None),) * 5 + (P("sx", "sy", None),) * 3
    return jax.shard_map(
        body,
        mesh=mesh,
        in_specs=placed,
        out_specs=(P("sx", "sy", None, None), P("sx", "sy", None, None)),
        check_vma=False,
    )
```

```python
import functools

import jax
import jax.numpy as jnp
from jax import lax
from jax.experimental import pallas as pl
from jax.experimental.pallas import tpu as pltpu
from jax.sharding import PartitionSpec as P

MROW = 64
ITERS = 3
CHUNKS = 4
RELAYED = ((), (-1, 0, 1), (0,), ())
LANES = 128
MESH = pl.DeviceIdType.MESH

directions = ((-1, -1), (-1, 0), (-1, 1), (0, -1), (0, 1), (1, -1), (1, 0), (1, 1))
send_order = (0, 2, 5, 7, 3, 4, 1, 6)
ring = (-2, -1, 1, 2)
centre = 1.6
spread = 1.4
f32 = jnp.float32
bf16 = jnp.bfloat16
NN = (((1,), (0,)), ((), ()))
TN = (((0,), (0,)), ((), ()))


def mm(left, right, dims=NN):
    return lax.dot_general(left, right, dims, preferred_element_type=f32)


def exact(left, right, dims=NN):
    return lax.dot_general(left, right, dims, precision=lax.Precision.HIGHEST, preferred_element_type=f32)


def split(value):
    high = value.astype(bf16)
    return high, (value - high.astype(f32)).astype(bf16)


def select_rows(value, one_hot):
    count = value.shape[0]
    both = mm(jnp.concatenate(split(value), axis=0), one_hot)
    return both[:count] + both[count:]


def iota(shape, axis):
    return lax.broadcasted_iota(jnp.int32, shape, axis)


def kernel(
    nx, ny,
    source, schur, inverse, basis, coarse, pmap, counts, order,
    sol_out, res_out,
    source_v, inverse_v, schur_v, gather, scatter, inverse_g, inverse_w, schur_g, schur_w, basis_q, picked_g, picked_w,
    cmat, weight, res, sol, direction, local, shared, operand, picks, out_buf, in_buf, relay_buf, prim_buf, maps, coarses,
    load_sem, out_send, out_recv, relay_send, relay_recv, prim_send, prim_recv, meta_send, meta_recv,
):
    me_x, me_y = lax.axis_index("sx"), lax.axis_index("sy")
    rows, width = source.shape[2], source.shape[3]
    block = coarse.shape[2]
    modes = basis.shape[2]
    slots = 8 * MROW
    links = len(ring)
    stages = 1 + 2 * ITERS
    wide = width // CHUNKS
    half = wide // 2
    parts = LANES // modes
    quarter = wide // parts

    def inside(d):
        a, b = directions[d]
        x, y = me_x + a, me_y + b
        return (x >= 0) & (x < nx) & (y >= 0) & (y < ny)

    def peer(d):
        a, b = directions[d]
        return (me_x + a, me_y + b)

    def ring_peer(s):
        return (lax.rem(me_x + s + nx, nx), me_y)

    load_source = pltpu.make_async_copy(source.at[0, 0], source_v, load_sem.at[0])
    load_inverse = pltpu.make_async_copy(inverse.at[0, 0], inverse_v, load_sem.at[1])
    load_schur = pltpu.make_async_copy(schur.at[0, 0], schur_v, load_sem.at[2])
    load_source.start()
    load_inverse.start()
    load_schur.start()

    barrier = pltpu.get_barrier_semaphore()
    total = jnp.int32(links)
    for d in range(8):
        total = total + inside(d).astype(jnp.int32)

        @pl.when(inside(d))
        def _(d=d):
            pl.semaphore_signal(barrier, inc=1, device_id=peer(d), device_id_type=MESH)

    for s in ring:
        pl.semaphore_signal(barrier, inc=1, device_id=ring_peer(s), device_id_type=MESH)

    turn = ny // 2
    paired = {turn - 1: (ny - 1, 0), ny - 1: (turn - 1, turn), turn: (0, ny - 1), 0: (turn, turn - 1)}
    for mine, (straight, fan) in paired.items():
        at = me_y == mine
        total = total + at.astype(jnp.int32)

        @pl.when(at)
        def _(straight=straight):
            pl.semaphore_signal(barrier, inc=1, device_id=(me_x, straight), device_id_type=MESH)

        for a in (-1, 0, 1):
            valid = at & (me_x + a >= 0) & (me_x + a < nx)
            total = total + valid.astype(jnp.int32)

            @pl.when(valid)
            def _(fan=fan, a=a):
                pl.semaphore_signal(barrier, inc=1, device_id=(me_x + a, fan), device_id_type=MESH)

    slot = iota((1, slots), 1)
    begins = jnp.zeros((1, slots), jnp.int32)
    sizes = jnp.zeros((1, slots), jnp.int32)
    start = jnp.int32(0)
    for d in range(8):
        count = counts[0, 0, d]
        mine = slot // MROW == d
        begins = jnp.where(mine, start, begins)
        sizes = jnp.where(mine, count, sizes)
        start = start + count
    place = lax.rem(slot, MROW)
    position = jnp.where(place < sizes, begins + place, -1)
    row_of = iota((rows, slots), 0)
    scatter[...] = jnp.where(row_of == position, 1.0, 0.0).astype(bf16)
    digit = iota((16, rows), 0)
    ids = order[0]
    digits = jnp.where(digit == 0, ids // 256, jnp.where(digit == 1, lax.rem(ids, 256), 1))
    found = mm(digits.astype(f32).astype(bf16), scatter[...])
    target = jnp.where(found[2:3] > 0.5, 256.0 * found[0:1] + found[1:2], -1.0)
    scatter[...] = jnp.where(row_of == target.astype(jnp.int32), 1.0, 0.0).astype(bf16)

    low_lanes = iota((half, LANES), 1) < MROW

    def out_copy(stage, c, d):
        return pltpu.make_async_remote_copy(
            src_ref=out_buf.at[d, stage, c],
            dst_ref=in_buf.at[7 - d, stage, c],
            send_sem=out_send.at[d],
            recv_sem=out_recv.at[stage % 2, c, 7 - d],
            device_id=peer(d),
            device_id_type=MESH,
        )

    def in_copy(stage, c, d):
        return pltpu.make_async_remote_copy(
            src_ref=out_buf.at[7 - d, stage, c],
            dst_ref=in_buf.at[d, stage, c],
            send_sem=out_send.at[7 - d],
            recv_sem=out_recv.at[stage % 2, c, d],
            device_id=peer(d),
            device_id_type=MESH,
        )

    def pack(stage, c, value):
        for t in range(slots // LANES):
            tile = value[:, t * LANES:(t + 1) * LANES]
            top, low = tile[:half], tile[half:]
            out_buf[2 * t, stage, c] = jnp.where(low_lanes, top, pltpu.roll(low, MROW, 1))
            out_buf[2 * t + 1, stage, c] = jnp.where(low_lanes, pltpu.roll(top, MROW, 1), low)

    def send_all(stage, c):
        for d in send_order:
            a, b = directions[d]
            direct = inside(d)
            if a in RELAYED[c] and b != 0:
                crossing = me_y == (turn - 1 if b > 0 else turn)

                @pl.when(inside(d) & crossing)
                def _(d=d, a=a, b=b):
                    pltpu.make_async_remote_copy(
                        src_ref=out_buf.at[d, stage, c],
                        dst_ref=relay_buf.at[a + 1, stage, c],
                        send_sem=out_send.at[d],
                        recv_sem=relay_recv.at[a + 1, stage % 2, c],
                        device_id=(me_x, ny - 1 if b > 0 else 0),
                        device_id_type=MESH,
                    ).start()

                direct = direct & jnp.logical_not(crossing)

            @pl.when(direct)
            def _(d=d):
                out_copy(stage, c, d).start()

    def relay(stage, c):
        if not RELAYED[c]:
            return
        for b in (1, -1):
            @pl.when(me_y == (ny - 1 if b > 0 else 0))
            def _(b=b):
                for a in RELAYED[c]:
                    @pl.when((me_x + a >= 0) & (me_x + a < nx))
                    def _(a=a):
                        slot = 7 - directions.index((a, b))
                        pltpu.make_async_remote_copy(
                            src_ref=relay_buf.at[a + 1, stage, c],
                            dst_ref=relay_buf.at[a + 1, stage, c],
                            send_sem=relay_send.at[a + 1],
                            recv_sem=relay_recv.at[a + 1, stage % 2, c],
                            device_id=(me_x, turn - 1 if b > 0 else turn),
                            device_id_type=MESH,
                        ).wait_recv()
                        pltpu.make_async_remote_copy(
                            src_ref=relay_buf.at[a + 1, stage, c],
                            dst_ref=in_buf.at[slot, stage, c],
                            send_sem=relay_send.at[a + 1],
                            recv_sem=out_recv.at[stage % 2, c, slot],
                            device_id=(me_x + a, turn if b > 0 else turn - 1),
                            device_id_type=MESH,
                        ).start()


    def wait_all(stage, c):
        for d in range(8):
            @pl.when(inside(d))
            def _(d=d):
                in_copy(stage, c, d).wait_recv()

    def relay_all(stage):
        for c in range(CHUNKS):
            relay(stage, c)

    def receive(stage, c):
        wait_all(stage, c)
        tops, lows = [], []
        for t in range(slots // LANES):
            first, second = in_buf[2 * t, stage, c], in_buf[2 * t + 1, stage, c]
            tops.append(jnp.where(low_lanes, first, pltpu.roll(second, MROW, 1)))
            lows.append(jnp.where(low_lanes, pltpu.roll(first, MROW, 1), second))
        value = jnp.concatenate([jnp.concatenate(tops, axis=1), jnp.concatenate(lows, axis=1)], axis=0)
        return select_rows(value, gather[...])

    def ring_copies(src, dst, send, recv):
        return [
            pltpu.make_async_remote_copy(
                src_ref=src, dst_ref=dst(links - 1 - at), send_sem=send(at), recv_sem=recv(links - 1 - at),
                device_id=ring_peer(s), device_id_type=MESH,
            )
            for at, s in enumerate(ring)
        ]

    def prim_copies(step, c):
        return ring_copies(
            prim_buf.at[links, step, c], lambda t: prim_buf.at[t, step, c],
            lambda t: prim_send.at[t], lambda t: prim_recv.at[step, c, t],
        )

    def chunk(c):
        return slice(c * wide, (c + 1) * wide)

    for d in range(8):
        @pl.when(jnp.logical_not(inside(d)))
        def _(d=d):
            in_buf[d] = jnp.zeros(in_buf.shape[1:], f32)

    map_copies = ring_copies(
        pmap.at[0, 0], lambda t: maps.at[t], lambda t: meta_send.at[0, t], lambda t: meta_recv.at[0, t]
    )
    coarse_copies = ring_copies(
        coarse.at[0, 0], lambda t: coarses.at[t], lambda t: meta_send.at[1, t], lambda t: meta_recv.at[1, t]
    )
    load_source.wait()
    for at in range(width // LANES):
        res[at * LANES:(at + 1) * LANES, :] = source_v[:, at * LANES:(at + 1) * LANES].T
    for c in range(CHUNKS):
        pack(0, c, select_rows(res[chunk(c), :], scatter[...]))
        if c == 0:
            pl.semaphore_wait(barrier, total)
            for copy in map_copies + coarse_copies:
                copy.start()
        send_all(0, c)

    column = jnp.broadcast_to(target, (8, slots)).T[:, 0:1].astype(jnp.int32)
    gather[...] = jnp.where(iota((slots, rows), 1) == column, 1.0, 0.0).astype(bf16)
    marks = mm(jnp.ones((16, slots), bf16), gather[...])
    weight[...] = 1.0 - 0.5 * marks[:8]
    scale = weight[0:1, :]
    halved = (scatter[...].astype(f32) * 0.5).astype(bf16)
    basis_t = basis[0, 0]
    basis_q[...] = jnp.concatenate([basis_t.astype(f32)] * parts, axis=0).T.astype(bf16)
    picked_g[...] = jnp.concatenate([mm(basis_t, halved)] * parts, axis=0).astype(bf16)
    picked_w[...] = jnp.concatenate([basis_t.astype(f32) * scale] * parts, axis=0).astype(bf16)
    relay_all(0)
    load_inverse.wait()
    inverse_w[...] = inverse_v[...].T
    inverse_g[...] = mm(inverse_w[...], halved).astype(bf16)
    inverse_w[...] = (inverse_w[...].astype(f32) * scale).astype(bf16)
    part_of = iota((quarter, LANES), 1) // modes

    def begin(step, c):
        scaled = (weight[0:1, :] * res[chunk(c), :]).astype(bf16)
        primal = mm(scaled, basis_q[...])
        packed = primal[:quarter]
        for q in range(1, parts):
            packed = jnp.where(part_of == q, primal[q * quarter:(q + 1) * quarter], packed)
        prim_buf[links, step, c] = packed
        for copy in prim_copies(step, c):
            copy.start()
        shared[chunk(c), :] = mm(scaled, inverse_g[...])
        operand[chunk(c), :] = scaled

    def wait_prim(step, c):
        for copy in prim_copies(step, c):
            copy.wait_recv()

    def finish(step, c):
        wait_prim(step, c)
        primal = jnp.concatenate([prim_buf[t, step, c] for t in range(links + 1)], axis=1)
        both = mm(jnp.concatenate(split(primal), axis=0), cmat[...])
        packed = both[:quarter, :LANES] + (both[quarter:, :LANES] + both[:quarter, LANES:])
        picked = jnp.concatenate(
            [jnp.where(part_of == q, packed, 0.0) for q in range(parts)], axis=0
        ).astype(bf16)
        pack(1 + 2 * step, c, shared[chunk(c), :] + mm(picked, picked_g[...]))
        send_all(1 + 2 * step, c)
        picks[chunk(c), :] = picked

    load_schur.wait()
    schur_w[...] = schur_v[...].T
    schur_g[...] = mm(schur_w[...], scatter[...]).astype(bf16)

    for copy in map_copies + coarse_copies:
        copy.wait_recv()

    slot_iota = iota((3 * block, modes), 0)

    def chooser(ids):
        relative = lax.rem(ids // block - me_x + 1 + 2 * nx, nx)
        place = relative * block + lax.rem(ids, block)
        return jnp.where(slot_iota == place, 1.0, 0.0).astype(f32)

    own = chooser(pmap[0, 0])
    blocks = (coarses[1], coarse[0, 0], coarses[2])
    chosen = jnp.concatenate([chooser(maps[t]) for t in range(links)] + [own], axis=1)
    solved = jnp.concatenate(
        [exact(blocks[t], chosen[t * block:(t + 1) * block, :]) for t in range(3)], axis=0
    )
    mapped = exact(solved, jnp.concatenate([own] * parts, axis=1), TN)
    same = iota((LANES, LANES), 0) // modes == iota((LANES, LANES), 1) // modes
    for t in range(links + 1):
        tiled = jnp.where(same, jnp.concatenate([mapped[t * modes:(t + 1) * modes]] * parts, axis=0), 0.0)
        high, low = split(tiled)
        cmat[t * LANES:(t + 1) * LANES, :LANES] = high
        cmat[t * LANES:(t + 1) * LANES, LANES:] = low

    for c in range(CHUNKS):
        res[chunk(c), :] = res[chunk(c), :] + receive(0, c)
        begin(0, c)

    sigma = centre / spread
    rho = 1.0 / sigma
    for step in range(ITERS):
        stage = 1 + 2 * step
        local[...] = mm(operand[...], inverse_w[...])
        for c in range(CHUNKS):
            finish(step, c)
        local[...] = local[...] + mm(picks[...], picked_w[...])
        if step > 0:
            rho_new = 1.0 / (2.0 * sigma - rho)
            keep, gain = rho_new * rho, 2.0 * rho_new / spread
            rho = rho_new
        relay_all(stage)
        for c in range(CHUNKS):
            update = local[chunk(c), :] + receive(stage, c)
            if step == 0:
                moved = update / centre
            else:
                moved = keep * direction[chunk(c), :] + gain * update
            direction[chunk(c), :] = moved
            rounded = moved.astype(bf16)
            operand[chunk(c), :] = rounded
            pack(stage + 1, c, mm(rounded, schur_g[...]))
            send_all(stage + 1, c)
        local[...] = mm(operand[...], schur_w[...])
        if step == 0:
            sol[...] = direction[...]
        else:
            sol[...] = sol[...] + direction[...]
        if step + 1 == ITERS:
            for at in range(width // LANES):
                sol_out[0, 0, :, at * LANES:(at + 1) * LANES] = sol[at * LANES:(at + 1) * LANES, :].T
        relay_all(stage + 1)
        for c in range(CHUNKS):
            res[chunk(c), :] = res[chunk(c), :] - (local[chunk(c), :] + receive(stage + 1, c))
            if step + 1 < ITERS:
                begin(step + 1, c)
            elif (c + 1) * wide % LANES == 0:
                at = (c + 1) * wide // LANES - 1
                res_out[0, 0, :, at * LANES:(at + 1) * LANES] = res[at * LANES:(at + 1) * LANES, :].T
    for copy in map_copies + coarse_copies:
        copy.wait_send()
    for at, s in enumerate(ring):
        pltpu.make_async_remote_copy(
            src_ref=prim_buf.at[links], dst_ref=prim_buf.at[links - 1 - at],
            send_sem=prim_send.at[at], recv_sem=prim_recv.at[0, 0, 0],
            device_id=ring_peer(s), device_id_type=MESH,
        ).wait_send()
    for a in (-1, 0, 1):
        ways = sum(a in chosen for chosen in RELAYED)

        @pl.when((ways > 0) & ((me_y == 0) | (me_y == ny - 1)) & (me_x + a >= 0) & (me_x + a < nx))
        def _(a=a):
            pltpu.make_async_remote_copy(
                src_ref=relay_buf.at[a + 1, :, pl.ds(0, ways)], dst_ref=relay_buf.at[a + 1, :, pl.ds(0, ways)],
                send_sem=relay_send.at[a + 1], recv_sem=relay_recv.at[a + 1, 0, 0],
                device_id=(me_x, turn), device_id_type=MESH,
            ).wait_send()
    for d in range(8):
        @pl.when(inside(d))
        def _(d=d):
            pltpu.make_async_remote_copy(
                src_ref=out_buf.at[d], dst_ref=in_buf.at[7 - d],
                send_sem=out_send.at[d], recv_sem=out_recv.at[0, 0, 0],
                device_id=peer(d), device_id_type=MESH,
            ).wait_send()


def deliver(sol, res, sol_out, res_out, sems):
    copies = [pltpu.make_async_copy(sol, sol_out, sems.at[0]), pltpu.make_async_copy(res, res_out, sems.at[1])]
    for copy in copies:
        copy.start()
    for copy in copies:
        copy.wait()


def solution(mesh):
    nx, ny = mesh.shape["sx"], mesh.shape["sy"]

    def body(source, schur, inverse, basis, coarse, pmap, counts, order):
        rows, width = source.shape[2:]
        modes, block = basis.shape[3], coarse.shape[2]
        slots, wide, stages, links = 8 * MROW, width // CHUNKS, 1 + 2 * ITERS, len(ring)
        half, quarter = wide // 2, wide * modes // LANES
        vmem = pl.BlockSpec(memory_space=pltpu.VMEM)
        hbm = pl.BlockSpec(memory_space=pl.ANY)
        smem = pl.BlockSpec(memory_space=pltpu.SMEM)
        dma = pltpu.SemaphoreType.DMA
        shape = jax.ShapeDtypeStruct(source.shape, f32)
        held = pltpu.VMEM(source.shape, f32)
        results = pl.pallas_call(
            functools.partial(kernel, nx, ny),
            out_shape=(held, held),
            in_specs=[hbm, hbm, hbm, vmem, vmem, vmem, smem, vmem],
            out_specs=(vmem, vmem),
            scratch_shapes=[
                pltpu.VMEM((rows, width), f32),
                pltpu.VMEM((rows, rows), bf16),
                pltpu.VMEM((rows, rows), bf16),
                pltpu.VMEM((slots, rows), bf16),
                pltpu.VMEM((rows, slots), bf16),
                pltpu.VMEM((rows, slots), bf16),
                pltpu.VMEM((rows, rows), bf16),
                pltpu.VMEM((rows, slots), bf16),
                pltpu.VMEM((rows, rows), bf16),
                pltpu.VMEM((rows, LANES), bf16),
                pltpu.VMEM((LANES, slots), bf16),
                pltpu.VMEM((LANES, rows), bf16),
                pltpu.VMEM(((links + 1) * LANES, 2 * LANES), bf16),
                pltpu.VMEM((8, rows), f32),
                pltpu.VMEM((width, rows), f32),
                pltpu.VMEM((width, rows), f32),
                pltpu.VMEM((width, rows), f32),
                pltpu.VMEM((width, rows), f32),
                pltpu.VMEM((width, slots), f32),
                pltpu.VMEM((width, rows), bf16),
                pltpu.VMEM((width, LANES), bf16),
                pltpu.VMEM((8, stages, CHUNKS, half, LANES), f32),
                pltpu.VMEM((8, stages, CHUNKS, half, LANES), f32),
                pltpu.VMEM((3, stages, CHUNKS, half, LANES), f32),
                pltpu.VMEM((links + 1, ITERS, CHUNKS, quarter, LANES), f32),
                pltpu.VMEM((links, 1, modes), jnp.int32),
                pltpu.VMEM((links, block, block), f32),
                dma((3,)),
                dma((8,)),
                dma((2, CHUNKS, 8)),
                dma((3,)),
                dma((3, 2, CHUNKS)),
                dma((links,)),
                dma((ITERS, CHUNKS, links)),
                dma((2, links)),
                dma((2, links)),
            ],
            compiler_params=pltpu.CompilerParams(
                collective_id=0, has_side_effects=True, vmem_limit_bytes=62 * 1024 * 1024
            ),
        )(source, schur, inverse, jnp.swapaxes(basis, 2, 3), coarse, pmap[:, :, None, :], counts, order)
        return pl.pallas_call(
            deliver,
            out_shape=(shape, shape),
            in_specs=[vmem, vmem],
            out_specs=(hbm, hbm),
            scratch_shapes=[dma((2,))],
            compiler_params=pltpu.CompilerParams(vmem_limit_bytes=1024 * 1024),
        )(*[pltpu.with_memory_space_constraint(value, pltpu.VMEM) for value in results])

    placed = (P("sx", "sy", None, None),) * 5 + (P("sx", "sy", None),) * 3
    return jax.shard_map(
        body,
        mesh=mesh,
        in_specs=placed,
        out_specs=(P("sx", "sy", None, None), P("sx", "sy", None, None)),
        check_vma=False,
    )
```

```python
import functools

import jax
import jax.numpy as jnp
from jax import lax
from jax.experimental import pallas as pl
from jax.experimental.pallas import tpu as pltpu
from jax.sharding import PartitionSpec as P

MROW = 64
ITERS = 3
CHUNKS = 4
RELAYED = (((), (-1, 0, 1), (-1, 0, 1), ()), ((), (-1, 0, 1), (-1, 0, 1), ()))
LANES = 128
MESH = pl.DeviceIdType.MESH

directions = ((-1, -1), (-1, 0), (-1, 1), (0, -1), (0, 1), (1, -1), (1, 0), (1, 1))
send_order = (0, 2, 5, 7, 3, 4, 1, 6)
ring = (-2, -1, 1, 2)
centre = 1.6
spread = 1.4
f32 = jnp.float32
bf16 = jnp.bfloat16
NN = (((1,), (0,)), ((), ()))
TN = (((0,), (0,)), ((), ()))


def mm(left, right, dims=NN):
    return lax.dot_general(left, right, dims, preferred_element_type=f32)


def exact(left, right, dims=NN):
    return lax.dot_general(left, right, dims, precision=lax.Precision.HIGHEST, preferred_element_type=f32)


def split(value):
    high = value.astype(bf16)
    return high, (value - high.astype(f32)).astype(bf16)


def select_rows(value, one_hot):
    count = value.shape[0]
    both = mm(jnp.concatenate(split(value), axis=0), one_hot)
    return both[:count] + both[count:]


def iota(shape, axis):
    return lax.broadcasted_iota(jnp.int32, shape, axis)


def kernel(
    nx, ny,
    source, schur, inverse, basis, coarse, pmap, counts, order,
    sol_out, res_out,
    source_v, inverse_v, schur_v, gather, scatter, inverse_g, inverse_w, schur_g, schur_w, basis_q, picked_g, picked_w,
    cmat, weight, res, sol, direction, local, shared, operand, picks, out_buf, in_buf, relay_buf, prim_buf, maps, coarses,
    load_sem, out_send, out_recv, relay_send, relay_recv, prim_send, prim_recv, meta_send, meta_recv,
):
    me_x, me_y = lax.axis_index("sx"), lax.axis_index("sy")
    rows, width = source.shape[2], source.shape[3]
    block = coarse.shape[2]
    modes = basis.shape[2]
    slots = 8 * MROW
    links = len(ring)
    stages = 1 + 2 * ITERS
    wide = width // CHUNKS
    half = wide // 2
    parts = LANES // modes
    quarter = wide // parts

    def inside(d):
        a, b = directions[d]
        x, y = me_x + a, me_y + b
        return (x >= 0) & (x < nx) & (y >= 0) & (y < ny)

    def peer(d):
        a, b = directions[d]
        return (me_x + a, me_y + b)

    def ring_peer(s):
        return (lax.rem(me_x + s + nx, nx), me_y)

    load_source = pltpu.make_async_copy(source.at[0, 0], source_v, load_sem.at[0])
    load_inverse = pltpu.make_async_copy(inverse.at[0, 0], inverse_v, load_sem.at[1])
    load_schur = pltpu.make_async_copy(schur.at[0, 0], schur_v, load_sem.at[2])
    load_source.start()
    load_inverse.start()
    load_schur.start()

    barrier = pltpu.get_barrier_semaphore()
    total = jnp.int32(links)
    for d in range(8):
        total = total + inside(d).astype(jnp.int32)

        @pl.when(inside(d))
        def _(d=d):
            pl.semaphore_signal(barrier, inc=1, device_id=peer(d), device_id_type=MESH)

    for s in ring:
        pl.semaphore_signal(barrier, inc=1, device_id=ring_peer(s), device_id_type=MESH)

    partner = me_x + 1 - 2 * lax.rem(me_x, 2)
    turn = ny // 2
    paired = {turn - 1: (ny - 1, 0), ny - 1: (turn - 1, turn), turn: (0, ny - 1), 0: (turn, turn - 1)}
    for mine, (straight, fan) in paired.items():
        at = me_y == mine
        total = total + 2 * at.astype(jnp.int32)

        @pl.when(at)
        def _(straight=straight):
            for x in (me_x, partner):
                pl.semaphore_signal(barrier, inc=1, device_id=(x, straight), device_id_type=MESH)

        for a in (-1, 0, 1):
            valid = at & (me_x + a >= 0) & (me_x + a < nx)
            total = total + valid.astype(jnp.int32)

            @pl.when(valid)
            def _(fan=fan, a=a):
                pl.semaphore_signal(barrier, inc=1, device_id=(me_x + a, fan), device_id_type=MESH)

    slot = iota((1, slots), 1)
    begins = jnp.zeros((1, slots), jnp.int32)
    sizes = jnp.zeros((1, slots), jnp.int32)
    start = jnp.int32(0)
    for d in range(8):
        count = counts[0, 0, d]
        mine = slot // MROW == d
        begins = jnp.where(mine, start, begins)
        sizes = jnp.where(mine, count, sizes)
        start = start + count
    place = lax.rem(slot, MROW)
    position = jnp.where(place < sizes, begins + place, -1)
    row_of = iota((rows, slots), 0)
    scatter[...] = jnp.where(row_of == position, 1.0, 0.0).astype(bf16)
    digit = iota((16, rows), 0)
    ids = order[0]
    digits = jnp.where(digit == 0, ids // 256, jnp.where(digit == 1, lax.rem(ids, 256), 1))
    found = mm(digits.astype(f32).astype(bf16), scatter[...])
    target = jnp.where(found[2:3] > 0.5, 256.0 * found[0:1] + found[1:2], -1.0)
    scatter[...] = jnp.where(row_of == target.astype(jnp.int32), 1.0, 0.0).astype(bf16)

    low_lanes = iota((half, LANES), 1) < MROW

    def out_copy(stage, c, d):
        return pltpu.make_async_remote_copy(
            src_ref=out_buf.at[d, stage, c],
            dst_ref=in_buf.at[7 - d, stage, c],
            send_sem=out_send.at[d],
            recv_sem=out_recv.at[stage % 2, c, 7 - d],
            device_id=peer(d),
            device_id_type=MESH,
        )

    def in_copy(stage, c, d):
        return pltpu.make_async_remote_copy(
            src_ref=out_buf.at[7 - d, stage, c],
            dst_ref=in_buf.at[d, stage, c],
            send_sem=out_send.at[7 - d],
            recv_sem=out_recv.at[stage % 2, c, d],
            device_id=peer(d),
            device_id_type=MESH,
        )

    def pack(stage, c, value):
        for t in range(slots // LANES):
            tile = value[:, t * LANES:(t + 1) * LANES]
            top, low = tile[:half], tile[half:]
            out_buf[2 * t, stage, c] = jnp.where(low_lanes, top, pltpu.roll(low, MROW, 1))
            out_buf[2 * t + 1, stage, c] = jnp.where(low_lanes, pltpu.roll(top, MROW, 1), low)

    def send_all(stage, c):
        for d in send_order:
            a, b = directions[d]
            direct = inside(d)
            if a in RELAYED[stage % 2][c] and b != 0:
                crossing = me_y == (turn - 1 if b > 0 else turn)

                @pl.when(inside(d) & crossing)
                def _(d=d, a=a, b=b):
                    pltpu.make_async_remote_copy(
                        src_ref=out_buf.at[d, stage, c],
                        dst_ref=relay_buf.at[a + 1, stage * CHUNKS + c],
                        send_sem=out_send.at[d],
                        recv_sem=relay_recv.at[a + 1, stage % 2, c],
                        device_id=(partner if a == 0 else me_x, ny - 1 if b > 0 else 0),
                        device_id_type=MESH,
                    ).start()

                direct = direct & jnp.logical_not(crossing)

            @pl.when(direct)
            def _(d=d):
                out_copy(stage, c, d).start()

    def relay(stage, c):
        if not RELAYED[stage % 2][c]:
            return
        for b in (1, -1):
            @pl.when(me_y == (ny - 1 if b > 0 else 0))
            def _(b=b):
                for a in RELAYED[stage % 2][c]:
                    home = partner if a == 0 else me_x

                    @pl.when((home + a >= 0) & (home + a < nx))
                    def _(a=a, home=home):
                        slot = 7 - directions.index((a, b))
                        pltpu.make_async_remote_copy(
                            src_ref=relay_buf.at[a + 1, stage * CHUNKS + c],
                            dst_ref=relay_buf.at[a + 1, stage * CHUNKS + c],
                            send_sem=relay_send.at[a + 1],
                            recv_sem=relay_recv.at[a + 1, stage % 2, c],
                            device_id=(home, turn - 1 if b > 0 else turn),
                            device_id_type=MESH,
                        ).wait_recv()
                        pltpu.make_async_remote_copy(
                            src_ref=relay_buf.at[a + 1, stage * CHUNKS + c],
                            dst_ref=in_buf.at[slot, stage, c],
                            send_sem=relay_send.at[a + 1],
                            recv_sem=out_recv.at[stage % 2, c, slot],
                            device_id=(home + a, turn if b > 0 else turn - 1),
                            device_id_type=MESH,
                        ).start()


    def wait_all(stage, c):
        for d in range(8):
            @pl.when(inside(d))
            def _(d=d):
                in_copy(stage, c, d).wait_recv()

    def relay_all(stage):
        for c in range(CHUNKS):
            relay(stage, c)

    def receive(stage, c):
        wait_all(stage, c)
        tops, lows = [], []
        for t in range(slots // LANES):
            first, second = in_buf[2 * t, stage, c], in_buf[2 * t + 1, stage, c]
            tops.append(jnp.where(low_lanes, first, pltpu.roll(second, MROW, 1)))
            lows.append(jnp.where(low_lanes, pltpu.roll(first, MROW, 1), second))
        value = jnp.concatenate([jnp.concatenate(tops, axis=1), jnp.concatenate(lows, axis=1)], axis=0)
        return select_rows(value, gather[...])

    def ring_copies(src, dst, send, recv):
        return [
            pltpu.make_async_remote_copy(
                src_ref=src, dst_ref=dst(links - 1 - at), send_sem=send(at), recv_sem=recv(links - 1 - at),
                device_id=ring_peer(s), device_id_type=MESH,
            )
            for at, s in enumerate(ring)
        ]

    def prim_copies(step, c):
        return ring_copies(
            prim_buf.at[links, step, c], lambda t: prim_buf.at[t, step, c],
            lambda t: prim_send.at[t], lambda t: prim_recv.at[step, c, t],
        )

    def chunk(c):
        return slice(c * wide, (c + 1) * wide)

    for d in range(8):
        @pl.when(jnp.logical_not(inside(d)))
        def _(d=d):
            in_buf[d] = jnp.zeros(in_buf.shape[1:], f32)

    map_copies = ring_copies(
        pmap.at[0, 0], lambda t: maps.at[t], lambda t: meta_send.at[0, t], lambda t: meta_recv.at[0, t]
    )
    coarse_copies = ring_copies(
        coarse.at[0, 0], lambda t: coarses.at[t], lambda t: meta_send.at[1, t], lambda t: meta_recv.at[1, t]
    )
    load_source.wait()
    for at in range(width // LANES):
        res[at * LANES:(at + 1) * LANES, :] = source_v[:, at * LANES:(at + 1) * LANES].T
    for c in range(CHUNKS):
        pack(0, c, select_rows(res[chunk(c), :], scatter[...]))
        if c == 0:
            pl.semaphore_wait(barrier, total)
            for copy in map_copies + coarse_copies:
                copy.start()
        send_all(0, c)

    column = jnp.broadcast_to(target, (8, slots)).T[:, 0:1].astype(jnp.int32)
    gather[...] = jnp.where(iota((slots, rows), 1) == column, 1.0, 0.0).astype(bf16)
    marks = mm(jnp.ones((16, slots), bf16), gather[...])
    weight[...] = 1.0 - 0.5 * marks[:8]
    scale = weight[0:1, :]
    halved = (scatter[...].astype(f32) * 0.5).astype(bf16)
    basis_t = basis[0, 0]
    basis_q[...] = jnp.concatenate([basis_t.astype(f32)] * parts, axis=0).T.astype(bf16)
    picked_g[...] = jnp.concatenate([mm(basis_t, halved)] * parts, axis=0).astype(bf16)
    picked_w[...] = jnp.concatenate([basis_t.astype(f32) * scale] * parts, axis=0).astype(bf16)
    load_inverse.wait()
    inverse_w[...] = inverse_v[...].T
    inverse_g[...] = mm(inverse_w[...], halved).astype(bf16)
    inverse_w[...] = (inverse_w[...].astype(f32) * scale).astype(bf16)
    part_of = iota((quarter, LANES), 1) // modes

    def begin(step, c):
        scaled = (weight[0:1, :] * res[chunk(c), :]).astype(bf16)
        primal = mm(scaled, basis_q[...])
        packed = primal[:quarter]
        for q in range(1, parts):
            packed = jnp.where(part_of == q, primal[q * quarter:(q + 1) * quarter], packed)
        prim_buf[links, step, c] = packed
        for copy in prim_copies(step, c):
            copy.start()
        shared[chunk(c), :] = mm(scaled, inverse_g[...])
        operand[chunk(c), :] = scaled

    def wait_prim(step, c):
        for copy in prim_copies(step, c):
            copy.wait_recv()

    def finish(step, c):
        wait_prim(step, c)
        primal = jnp.concatenate([prim_buf[t, step, c] for t in range(links + 1)], axis=1)
        both = mm(jnp.concatenate(split(primal), axis=0), cmat[...])
        packed = both[:quarter, :LANES] + (both[quarter:, :LANES] + both[:quarter, LANES:])
        picked = jnp.concatenate(
            [jnp.where(part_of == q, packed, 0.0) for q in range(parts)], axis=0
        ).astype(bf16)
        pack(1 + 2 * step, c, shared[chunk(c), :] + mm(picked, picked_g[...]))
        send_all(1 + 2 * step, c)
        picks[chunk(c), :] = picked

    load_schur.wait()
    schur_w[...] = schur_v[...].T
    schur_g[...] = mm(schur_w[...], scatter[...]).astype(bf16)

    relay_all(0)
    for copy in map_copies + coarse_copies:
        copy.wait_recv()

    slot_iota = iota((3 * block, modes), 0)

    def chooser(ids):
        relative = lax.rem(ids // block - me_x + 1 + 2 * nx, nx)
        place = relative * block + lax.rem(ids, block)
        return jnp.where(slot_iota == place, 1.0, 0.0).astype(f32)

    own = chooser(pmap[0, 0])
    blocks = (coarses[1], coarse[0, 0], coarses[2])
    chosen = jnp.concatenate([chooser(maps[t]) for t in range(links)] + [own], axis=1)
    solved = jnp.concatenate(
        [exact(blocks[t], chosen[t * block:(t + 1) * block, :]) for t in range(3)], axis=0
    )
    mapped = exact(solved, jnp.concatenate([own] * parts, axis=1), TN)
    same = iota((LANES, LANES), 0) // modes == iota((LANES, LANES), 1) // modes
    for t in range(links + 1):
        tiled = jnp.where(same, jnp.concatenate([mapped[t * modes:(t + 1) * modes]] * parts, axis=0), 0.0)
        high, low = split(tiled)
        cmat[t * LANES:(t + 1) * LANES, :LANES] = high
        cmat[t * LANES:(t + 1) * LANES, LANES:] = low

    for c in range(CHUNKS):
        res[chunk(c), :] = res[chunk(c), :] + receive(0, c)
        begin(0, c)

    sigma = centre / spread
    rho = 1.0 / sigma
    for step in range(ITERS):
        stage = 1 + 2 * step
        for c in range(CHUNKS):
            finish(step, c)
        local[...] = mm(operand[...], inverse_w[...]) + mm(picks[...], picked_w[...])
        if step > 0:
            rho_new = 1.0 / (2.0 * sigma - rho)
            keep, gain = rho_new * rho, 2.0 * rho_new / spread
            rho = rho_new
        relay_all(stage)
        for c in range(CHUNKS):
            update = local[chunk(c), :] + receive(stage, c)
            if step == 0:
                moved = update / centre
            else:
                moved = keep * direction[chunk(c), :] + gain * update
            direction[chunk(c), :] = moved
            rounded = moved.astype(bf16)
            operand[chunk(c), :] = rounded
            pack(stage + 1, c, mm(rounded, schur_g[...]))
            send_all(stage + 1, c)
        local[...] = mm(operand[...], schur_w[...])
        if step == 0:
            sol[...] = direction[...]
        else:
            sol[...] = sol[...] + direction[...]
        if step + 1 == ITERS:
            for at in range(width // LANES):
                sol_out[0, 0, :, at * LANES:(at + 1) * LANES] = sol[at * LANES:(at + 1) * LANES, :].T
        relay_all(stage + 1)
        for c in range(CHUNKS):
            res[chunk(c), :] = res[chunk(c), :] - (local[chunk(c), :] + receive(stage + 1, c))
            if step + 1 < ITERS:
                begin(step + 1, c)
            elif (c + 1) * wide % LANES == 0:
                at = (c + 1) * wide // LANES - 1
                res_out[0, 0, :, at * LANES:(at + 1) * LANES] = res[at * LANES:(at + 1) * LANES, :].T
    for copy in map_copies + coarse_copies:
        copy.wait_send()
    for at, s in enumerate(ring):
        pltpu.make_async_remote_copy(
            src_ref=prim_buf.at[links], dst_ref=prim_buf.at[links - 1 - at],
            send_sem=prim_send.at[at], recv_sem=prim_recv.at[0, 0, 0],
            device_id=ring_peer(s), device_id_type=MESH,
        ).wait_send()
    for a in (-1, 0, 1):
        ways = sum(a in chosen for stage in range(stages) for chosen in RELAYED[stage % 2])

        @pl.when((ways > 0) & ((me_y == 0) | (me_y == ny - 1)) & (me_x + a >= 0) & (me_x + a < nx))
        def _(a=a):
            pltpu.make_async_remote_copy(
                src_ref=relay_buf.at[a + 1, pl.ds(0, ways)], dst_ref=relay_buf.at[a + 1, pl.ds(0, ways)],
                send_sem=relay_send.at[a + 1], recv_sem=relay_recv.at[a + 1, 0, 0],
                device_id=(me_x, turn), device_id_type=MESH,
            ).wait_send()
    for d in range(8):
        @pl.when(inside(d))
        def _(d=d):
            pltpu.make_async_remote_copy(
                src_ref=out_buf.at[d], dst_ref=in_buf.at[7 - d],
                send_sem=out_send.at[d], recv_sem=out_recv.at[0, 0, 0],
                device_id=peer(d), device_id_type=MESH,
            ).wait_send()


def deliver(sol, res, sol_out, res_out, sems):
    copies = [pltpu.make_async_copy(sol, sol_out, sems.at[0]), pltpu.make_async_copy(res, res_out, sems.at[1])]
    for copy in copies:
        copy.start()
    for copy in copies:
        copy.wait()


def solution(mesh):
    nx, ny = mesh.shape["sx"], mesh.shape["sy"]

    def body(source, schur, inverse, basis, coarse, pmap, counts, order):
        rows, width = source.shape[2:]
        modes, block = basis.shape[3], coarse.shape[2]
        slots, wide, stages, links = 8 * MROW, width // CHUNKS, 1 + 2 * ITERS, len(ring)
        half, quarter = wide // 2, wide * modes // LANES
        vmem = pl.BlockSpec(memory_space=pltpu.VMEM)
        hbm = pl.BlockSpec(memory_space=pl.ANY)
        smem = pl.BlockSpec(memory_space=pltpu.SMEM)
        dma = pltpu.SemaphoreType.DMA
        shape = jax.ShapeDtypeStruct(source.shape, f32)
        held = pltpu.VMEM(source.shape, f32)
        results = pl.pallas_call(
            functools.partial(kernel, nx, ny),
            out_shape=(held, held),
            in_specs=[hbm, hbm, hbm, vmem, vmem, vmem, smem, vmem],
            out_specs=(vmem, vmem),
            scratch_shapes=[
                pltpu.VMEM((rows, width), f32),
                pltpu.VMEM((rows, rows), bf16),
                pltpu.VMEM((rows, rows), bf16),
                pltpu.VMEM((slots, rows), bf16),
                pltpu.VMEM((rows, slots), bf16),
                pltpu.VMEM((rows, slots), bf16),
                pltpu.VMEM((rows, rows), bf16),
                pltpu.VMEM((rows, slots), bf16),
                pltpu.VMEM((rows, rows), bf16),
                pltpu.VMEM((rows, LANES), bf16),
                pltpu.VMEM((LANES, slots), bf16),
                pltpu.VMEM((LANES, rows), bf16),
                pltpu.VMEM(((links + 1) * LANES, 2 * LANES), bf16),
                pltpu.VMEM((8, rows), f32),
                pltpu.VMEM((width, rows), f32),
                pltpu.VMEM((width, rows), f32),
                pltpu.VMEM((width, rows), f32),
                pltpu.VMEM((width, rows), f32),
                pltpu.VMEM((width, slots), f32),
                pltpu.VMEM((width, rows), bf16),
                pltpu.VMEM((width, LANES), bf16),
                pltpu.VMEM((8, stages, CHUNKS, half, LANES), f32),
                pltpu.VMEM((8, stages, CHUNKS, half, LANES), f32),
                pltpu.VMEM((3, stages * CHUNKS, half, LANES), f32),
                pltpu.VMEM((links + 1, ITERS, CHUNKS, quarter, LANES), f32),
                pltpu.VMEM((links, 1, modes), jnp.int32),
                pltpu.VMEM((links, block, block), f32),
                dma((3,)),
                dma((8,)),
                dma((2, CHUNKS, 8)),
                dma((3,)),
                dma((3, 2, CHUNKS)),
                dma((links,)),
                dma((ITERS, CHUNKS, links)),
                dma((2, links)),
                dma((2, links)),
            ],
            compiler_params=pltpu.CompilerParams(
                collective_id=0, has_side_effects=True, vmem_limit_bytes=62 * 1024 * 1024
            ),
        )(source, schur, inverse, jnp.swapaxes(basis, 2, 3), coarse, pmap[:, :, None, :], counts, order)
        return pl.pallas_call(
            deliver,
            out_shape=(shape, shape),
            in_specs=[vmem, vmem],
            out_specs=(hbm, hbm),
            scratch_shapes=[dma((2,))],
            compiler_params=pltpu.CompilerParams(vmem_limit_bytes=1024 * 1024),
        )(*[pltpu.with_memory_space_constraint(value, pltpu.VMEM) for value in results])

    placed = (P("sx", "sy", None, None),) * 5 + (P("sx", "sy", None),) * 3
    return jax.shard_map(
        body,
        mesh=mesh,
        in_specs=placed,
        out_specs=(P("sx", "sy", None, None), P("sx", "sy", None, None)),
        check_vma=False,
    )
```

```python
import functools

import jax
import jax.numpy as jnp
from jax import lax
from jax.experimental import pallas as pl
from jax.experimental.pallas import tpu as pltpu
from jax.sharding import PartitionSpec as P

MROW = 64
ITERS = 3
CHUNKS = 4
RELAYED = (((), (-1, 1), (-1, 0, 1), (0,)), ((), (-1, 1), (-1, 0, 1), (0,)))
FORWARDS = ((1, 2), (3,), (), ())
LANES = 128
MESH = pl.DeviceIdType.MESH

directions = ((-1, -1), (-1, 0), (-1, 1), (0, -1), (0, 1), (1, -1), (1, 0), (1, 1))
send_order = (0, 2, 5, 7, 3, 4, 1, 6)
ring = (-2, -1, 1, 2)
centre = 1.6
spread = 1.4
f32 = jnp.float32
bf16 = jnp.bfloat16
NN = (((1,), (0,)), ((), ()))
TN = (((0,), (0,)), ((), ()))


def mm(left, right, dims=NN):
    return lax.dot_general(left, right, dims, preferred_element_type=f32)


def exact(left, right, dims=NN):
    return lax.dot_general(left, right, dims, precision=lax.Precision.HIGHEST, preferred_element_type=f32)


def split(value):
    high = value.astype(bf16)
    return high, (value - high.astype(f32)).astype(bf16)


def select_rows(value, one_hot):
    count = value.shape[0]
    both = mm(jnp.concatenate(split(value), axis=0), one_hot)
    return both[:count] + both[count:]


def iota(shape, axis):
    return lax.broadcasted_iota(jnp.int32, shape, axis)


def kernel(
    nx, ny,
    source, schur, inverse, basis, coarse, pmap, counts, order,
    sol_out, res_out,
    source_v, inverse_v, schur_v, gather, scatter, inverse_g, inverse_w, schur_g, schur_w, basis_q, picked_g, picked_w,
    cmat, weight, res, sol, direction, local, shared, operand, picks, out_buf, in_buf, relay_buf, prim_buf, maps, coarses,
    load_sem, out_send, out_recv, relay_send, relay_recv, prim_send, prim_recv, meta_send, meta_recv,
):
    me_x, me_y = lax.axis_index("sx"), lax.axis_index("sy")
    rows, width = source.shape[2], source.shape[3]
    block = coarse.shape[2]
    modes = basis.shape[2]
    slots = 8 * MROW
    links = len(ring)
    stages = 1 + 2 * ITERS
    wide = width // CHUNKS
    half = wide // 2
    parts = LANES // modes
    quarter = wide // parts

    def inside(d):
        a, b = directions[d]
        x, y = me_x + a, me_y + b
        return (x >= 0) & (x < nx) & (y >= 0) & (y < ny)

    def peer(d):
        a, b = directions[d]
        return (me_x + a, me_y + b)

    def ring_peer(s):
        return (lax.rem(me_x + s + nx, nx), me_y)

    load_source = pltpu.make_async_copy(source.at[0, 0], source_v, load_sem.at[0])
    load_inverse = pltpu.make_async_copy(inverse.at[0, 0], inverse_v, load_sem.at[1])
    load_schur = pltpu.make_async_copy(schur.at[0, 0], schur_v, load_sem.at[2])
    load_source.start()
    load_inverse.start()
    load_schur.start()

    barrier = pltpu.get_barrier_semaphore()
    total = jnp.int32(links)
    for d in range(8):
        total = total + inside(d).astype(jnp.int32)

        @pl.when(inside(d))
        def _(d=d):
            pl.semaphore_signal(barrier, inc=1, device_id=peer(d), device_id_type=MESH)

    for s in ring:
        pl.semaphore_signal(barrier, inc=1, device_id=ring_peer(s), device_id_type=MESH)

    partner = me_x + 1 - 2 * lax.rem(me_x, 2)
    turn = ny // 2
    paired = {turn - 1: (ny - 1, 0), ny - 1: (turn - 1, turn), turn: (0, ny - 1), 0: (turn, turn - 1)}
    for mine, (straight, fan) in paired.items():
        at = me_y == mine
        total = total + 2 * at.astype(jnp.int32)

        @pl.when(at)
        def _(straight=straight):
            for x in (me_x, partner):
                pl.semaphore_signal(barrier, inc=1, device_id=(x, straight), device_id_type=MESH)

        for a in (-1, 0, 1):
            valid = at & (me_x + a >= 0) & (me_x + a < nx)
            total = total + valid.astype(jnp.int32)

            @pl.when(valid)
            def _(fan=fan, a=a):
                pl.semaphore_signal(barrier, inc=1, device_id=(me_x + a, fan), device_id_type=MESH)

    slot = iota((1, slots), 1)
    begins = jnp.zeros((1, slots), jnp.int32)
    sizes = jnp.zeros((1, slots), jnp.int32)
    start = jnp.int32(0)
    for d in range(8):
        count = counts[0, 0, d]
        mine = slot // MROW == d
        begins = jnp.where(mine, start, begins)
        sizes = jnp.where(mine, count, sizes)
        start = start + count
    place = lax.rem(slot, MROW)
    position = jnp.where(place < sizes, begins + place, -1)
    row_of = iota((rows, slots), 0)
    scatter[...] = jnp.where(row_of == position, 1.0, 0.0).astype(bf16)
    digit = iota((16, rows), 0)
    ids = order[0]
    digits = jnp.where(digit == 0, ids // 256, jnp.where(digit == 1, lax.rem(ids, 256), 1))
    found = mm(digits.astype(f32).astype(bf16), scatter[...])
    target = jnp.where(found[2:3] > 0.5, 256.0 * found[0:1] + found[1:2], -1.0)
    scatter[...] = jnp.where(row_of == target.astype(jnp.int32), 1.0, 0.0).astype(bf16)

    low_lanes = iota((half, LANES), 1) < MROW

    def out_copy(stage, c, d):
        return pltpu.make_async_remote_copy(
            src_ref=out_buf.at[d, stage, c],
            dst_ref=in_buf.at[7 - d, stage, c],
            send_sem=out_send.at[d],
            recv_sem=out_recv.at[stage % 2, c, 7 - d],
            device_id=peer(d),
            device_id_type=MESH,
        )

    def in_copy(stage, c, d):
        return pltpu.make_async_remote_copy(
            src_ref=out_buf.at[7 - d, stage, c],
            dst_ref=in_buf.at[d, stage, c],
            send_sem=out_send.at[7 - d],
            recv_sem=out_recv.at[stage % 2, c, d],
            device_id=peer(d),
            device_id_type=MESH,
        )

    def pack(stage, c, value):
        for t in range(slots // LANES):
            tile = value[:, t * LANES:(t + 1) * LANES]
            top, low = tile[:half], tile[half:]
            out_buf[2 * t, stage, c] = jnp.where(low_lanes, top, pltpu.roll(low, MROW, 1))
            out_buf[2 * t + 1, stage, c] = jnp.where(low_lanes, pltpu.roll(top, MROW, 1), low)

    def send_all(stage, c):
        for d in send_order:
            a, b = directions[d]
            direct = inside(d)
            if a in RELAYED[stage % 2][c] and b != 0:
                crossing = me_y == (turn - 1 if b > 0 else turn)

                @pl.when(inside(d) & crossing)
                def _(d=d, a=a, b=b):
                    pltpu.make_async_remote_copy(
                        src_ref=out_buf.at[d, stage, c],
                        dst_ref=relay_buf.at[a + 1, stage * CHUNKS + c],
                        send_sem=out_send.at[d],
                        recv_sem=relay_recv.at[a + 1, stage % 2, c],
                        device_id=(partner if a == 0 else me_x, ny - 1 if b > 0 else 0),
                        device_id_type=MESH,
                    ).start()

                direct = direct & jnp.logical_not(crossing)

            @pl.when(direct)
            def _(d=d):
                out_copy(stage, c, d).start()

    def relay(stage, c):
        if not RELAYED[stage % 2][c]:
            return
        for b in (1, -1):
            @pl.when(me_y == (ny - 1 if b > 0 else 0))
            def _(b=b):
                for a in RELAYED[stage % 2][c]:
                    home = partner if a == 0 else me_x

                    @pl.when((home + a >= 0) & (home + a < nx))
                    def _(a=a, home=home):
                        slot = 7 - directions.index((a, b))
                        pltpu.make_async_remote_copy(
                            src_ref=relay_buf.at[a + 1, stage * CHUNKS + c],
                            dst_ref=relay_buf.at[a + 1, stage * CHUNKS + c],
                            send_sem=relay_send.at[a + 1],
                            recv_sem=relay_recv.at[a + 1, stage % 2, c],
                            device_id=(home, turn - 1 if b > 0 else turn),
                            device_id_type=MESH,
                        ).wait_recv()
                        pltpu.make_async_remote_copy(
                            src_ref=relay_buf.at[a + 1, stage * CHUNKS + c],
                            dst_ref=in_buf.at[slot, stage, c],
                            send_sem=relay_send.at[a + 1],
                            recv_sem=out_recv.at[stage % 2, c, slot],
                            device_id=(home + a, turn if b > 0 else turn - 1),
                            device_id_type=MESH,
                        ).start()


    def wait_all(stage, c):
        for d in range(8):
            @pl.when(inside(d))
            def _(d=d):
                in_copy(stage, c, d).wait_recv()

    def relay_all(stage):
        for c in range(CHUNKS):
            relay(stage, c)

    def forward(stage, place):
        for c in FORWARDS[place]:
            relay(stage, c)

    def receive(stage, c):
        wait_all(stage, c)
        tops, lows = [], []
        for t in range(slots // LANES):
            first, second = in_buf[2 * t, stage, c], in_buf[2 * t + 1, stage, c]
            tops.append(jnp.where(low_lanes, first, pltpu.roll(second, MROW, 1)))
            lows.append(jnp.where(low_lanes, pltpu.roll(first, MROW, 1), second))
        value = jnp.concatenate([jnp.concatenate(tops, axis=1), jnp.concatenate(lows, axis=1)], axis=0)
        return select_rows(value, gather[...])

    def ring_copies(src, dst, send, recv):
        return [
            pltpu.make_async_remote_copy(
                src_ref=src, dst_ref=dst(links - 1 - at), send_sem=send(at), recv_sem=recv(links - 1 - at),
                device_id=ring_peer(s), device_id_type=MESH,
            )
            for at, s in enumerate(ring)
        ]

    def prim_copies(step, c):
        return ring_copies(
            prim_buf.at[step, c, links], lambda t: prim_buf.at[step, c, t],
            lambda t: prim_send.at[t], lambda t: prim_recv.at[step, c],
        )

    def chunk(c):
        return slice(c * wide, (c + 1) * wide)

    for d in range(8):
        @pl.when(jnp.logical_not(inside(d)))
        def _(d=d):
            in_buf[d] = jnp.zeros(in_buf.shape[1:], f32)

    map_copies = ring_copies(
        pmap.at[0, 0], lambda t: maps.at[t], lambda t: meta_send.at[0, t], lambda t: meta_recv.at[0, t]
    )
    coarse_copies = ring_copies(
        coarse.at[0, 0], lambda t: coarses.at[t], lambda t: meta_send.at[1, t], lambda t: meta_recv.at[1, t]
    )
    load_source.wait()
    for at in range(width // LANES):
        res[at * LANES:(at + 1) * LANES, :] = source_v[:, at * LANES:(at + 1) * LANES].T
    for c in range(CHUNKS):
        pack(0, c, select_rows(res[chunk(c), :], scatter[...]))
        if c == 0:
            pl.semaphore_wait(barrier, total)
            for copy in map_copies + coarse_copies:
                copy.start()
        send_all(0, c)

    column = jnp.broadcast_to(target, (8, slots)).T[:, 0:1].astype(jnp.int32)
    gather[...] = jnp.where(iota((slots, rows), 1) == column, 1.0, 0.0).astype(bf16)
    marks = mm(jnp.ones((16, slots), bf16), gather[...])
    weight[...] = 1.0 - 0.5 * marks[:8]
    scale = weight[0:1, :]
    halved = (scatter[...].astype(f32) * 0.5).astype(bf16)
    basis_t = basis[0, 0]
    basis_q[...] = jnp.concatenate([basis_t.astype(f32)] * parts, axis=0).T.astype(bf16)
    picked_g[...] = jnp.concatenate([mm(basis_t, halved)] * parts, axis=0).astype(bf16)
    picked_w[...] = jnp.concatenate([basis_t.astype(f32) * scale] * parts, axis=0).astype(bf16)
    load_inverse.wait()
    inverse_w[...] = inverse_v[...].T
    inverse_g[...] = mm(inverse_w[...], halved).astype(bf16)
    inverse_w[...] = (inverse_w[...].astype(f32) * scale).astype(bf16)
    part_of = iota((quarter, LANES), 1) // modes

    def begin(step, c):
        scaled = (weight[0:1, :] * res[chunk(c), :]).astype(bf16)
        primal = mm(scaled, basis_q[...])
        packed = primal[:quarter]
        for q in range(1, parts):
            packed = jnp.where(part_of == q, primal[q * quarter:(q + 1) * quarter], packed)
        prim_buf[step, c, links] = packed
        for copy in prim_copies(step, c):
            copy.start()
        shared[chunk(c), :] = mm(scaled, inverse_g[...])
        operand[chunk(c), :] = scaled

    def wait_prim(step, c):
        arrived = prim_buf.at[step, c, pl.ds(0, links)]
        pltpu.make_async_remote_copy(
            src_ref=arrived, dst_ref=arrived, send_sem=prim_send.at[0], recv_sem=prim_recv.at[step, c],
            device_id=ring_peer(1), device_id_type=MESH,
        ).wait_recv()

    def finish(step, c):
        wait_prim(step, c)
        primal = jnp.concatenate([prim_buf[step, c, t] for t in range(links + 1)], axis=1)
        both = mm(jnp.concatenate(split(primal), axis=0), cmat[...])
        packed = both[:quarter, :LANES] + (both[quarter:, :LANES] + both[:quarter, LANES:])
        picked = jnp.concatenate(
            [jnp.where(part_of == q, packed, 0.0) for q in range(parts)], axis=0
        ).astype(bf16)
        pack(1 + 2 * step, c, shared[chunk(c), :] + mm(picked, picked_g[...]))
        send_all(1 + 2 * step, c)
        picks[chunk(c), :] = picked

    load_schur.wait()
    schur_w[...] = schur_v[...].T
    schur_g[...] = mm(schur_w[...], scatter[...]).astype(bf16)

    relay_all(0)
    for copy in map_copies + coarse_copies:
        copy.wait_recv()

    slot_iota = iota((3 * block, modes), 0)

    def chooser(ids):
        relative = lax.rem(ids // block - me_x + 1 + 2 * nx, nx)
        place = relative * block + lax.rem(ids, block)
        return jnp.where(slot_iota == place, 1.0, 0.0).astype(f32)

    own = chooser(pmap[0, 0])
    blocks = (coarses[1], coarse[0, 0], coarses[2])
    chosen = jnp.concatenate([chooser(maps[t]) for t in range(links)] + [own], axis=1)
    solved = jnp.concatenate(
        [exact(blocks[t], chosen[t * block:(t + 1) * block, :]) for t in range(3)], axis=0
    )
    mapped = exact(solved, jnp.concatenate([own] * parts, axis=1), TN)
    same = iota((LANES, LANES), 0) // modes == iota((LANES, LANES), 1) // modes
    for t in range(links + 1):
        tiled = jnp.where(same, jnp.concatenate([mapped[t * modes:(t + 1) * modes]] * parts, axis=0), 0.0)
        high, low = split(tiled)
        cmat[t * LANES:(t + 1) * LANES, :LANES] = high
        cmat[t * LANES:(t + 1) * LANES, LANES:] = low

    for c in range(CHUNKS):
        res[chunk(c), :] = res[chunk(c), :] + receive(0, c)
        begin(0, c)

    sigma = centre / spread
    rho = 1.0 / sigma
    for step in range(ITERS):
        stage = 1 + 2 * step
        for c in range(CHUNKS):
            finish(step, c)
        local[...] = mm(operand[...], inverse_w[...]) + mm(picks[...], picked_w[...])
        if step > 0:
            rho_new = 1.0 / (2.0 * sigma - rho)
            keep, gain = rho_new * rho, 2.0 * rho_new / spread
            rho = rho_new
        for c in range(CHUNKS):
            forward(stage, c)
            update = local[chunk(c), :] + receive(stage, c)
            if step == 0:
                moved = update / centre
            else:
                moved = keep * direction[chunk(c), :] + gain * update
            direction[chunk(c), :] = moved
            rounded = moved.astype(bf16)
            operand[chunk(c), :] = rounded
            pack(stage + 1, c, mm(rounded, schur_g[...]))
            send_all(stage + 1, c)
        local[...] = mm(operand[...], schur_w[...])
        if step == 0:
            sol[...] = direction[...]
        else:
            sol[...] = sol[...] + direction[...]
        if step + 1 == ITERS:
            for at in range(width // LANES):
                sol_out[0, 0, :, at * LANES:(at + 1) * LANES] = sol[at * LANES:(at + 1) * LANES, :].T
        for c in range(CHUNKS):
            forward(stage + 1, c)
            res[chunk(c), :] = res[chunk(c), :] - (local[chunk(c), :] + receive(stage + 1, c))
            if step + 1 < ITERS:
                begin(step + 1, c)
            elif (c + 1) * wide % LANES == 0:
                at = (c + 1) * wide // LANES - 1
                res_out[0, 0, :, at * LANES:(at + 1) * LANES] = res[at * LANES:(at + 1) * LANES, :].T
    for copy in map_copies + coarse_copies:
        copy.wait_send()
    for at, s in enumerate(ring):
        pltpu.make_async_remote_copy(
            src_ref=prim_buf.at[:, :, links], dst_ref=prim_buf.at[:, :, links - 1 - at],
            send_sem=prim_send.at[at], recv_sem=prim_recv.at[0, 0],
            device_id=ring_peer(s), device_id_type=MESH,
        ).wait_send()
    for a in (-1, 0, 1):
        ways = sum(a in chosen for stage in range(stages) for chosen in RELAYED[stage % 2])

        @pl.when((ways > 0) & ((me_y == 0) | (me_y == ny - 1)) & (me_x + a >= 0) & (me_x + a < nx))
        def _(a=a):
            pltpu.make_async_remote_copy(
                src_ref=relay_buf.at[a + 1, pl.ds(0, ways)], dst_ref=relay_buf.at[a + 1, pl.ds(0, ways)],
                send_sem=relay_send.at[a + 1], recv_sem=relay_recv.at[a + 1, 0, 0],
                device_id=(me_x, turn), device_id_type=MESH,
            ).wait_send()
    for d in range(8):
        @pl.when(inside(d))
        def _(d=d):
            pltpu.make_async_remote_copy(
                src_ref=out_buf.at[d], dst_ref=in_buf.at[7 - d],
                send_sem=out_send.at[d], recv_sem=out_recv.at[0, 0, 0],
                device_id=peer(d), device_id_type=MESH,
            ).wait_send()


def deliver(sol, res, sol_out, res_out, sems):
    copies = [pltpu.make_async_copy(sol, sol_out, sems.at[0]), pltpu.make_async_copy(res, res_out, sems.at[1])]
    for copy in copies:
        copy.start()
    for copy in copies:
        copy.wait()


def solution(mesh):
    nx, ny = mesh.shape["sx"], mesh.shape["sy"]

    def body(source, schur, inverse, basis, coarse, pmap, counts, order):
        rows, width = source.shape[2:]
        modes, block = basis.shape[3], coarse.shape[2]
        slots, wide, stages, links = 8 * MROW, width // CHUNKS, 1 + 2 * ITERS, len(ring)
        half, quarter = wide // 2, wide * modes // LANES
        vmem = pl.BlockSpec(memory_space=pltpu.VMEM)
        hbm = pl.BlockSpec(memory_space=pl.ANY)
        smem = pl.BlockSpec(memory_space=pltpu.SMEM)
        dma = pltpu.SemaphoreType.DMA
        shape = jax.ShapeDtypeStruct(source.shape, f32)
        held = pltpu.VMEM(source.shape, f32)
        results = pl.pallas_call(
            functools.partial(kernel, nx, ny),
            out_shape=(held, held),
            in_specs=[hbm, hbm, hbm, vmem, vmem, vmem, smem, vmem],
            out_specs=(vmem, vmem),
            scratch_shapes=[
                pltpu.VMEM((rows, width), f32),
                pltpu.VMEM((rows, rows), bf16),
                pltpu.VMEM((rows, rows), bf16),
                pltpu.VMEM((slots, rows), bf16),
                pltpu.VMEM((rows, slots), bf16),
                pltpu.VMEM((rows, slots), bf16),
                pltpu.VMEM((rows, rows), bf16),
                pltpu.VMEM((rows, slots), bf16),
                pltpu.VMEM((rows, rows), bf16),
                pltpu.VMEM((rows, LANES), bf16),
                pltpu.VMEM((LANES, slots), bf16),
                pltpu.VMEM((LANES, rows), bf16),
                pltpu.VMEM(((links + 1) * LANES, 2 * LANES), bf16),
                pltpu.VMEM((8, rows), f32),
                pltpu.VMEM((width, rows), f32),
                pltpu.VMEM((width, rows), f32),
                pltpu.VMEM((width, rows), f32),
                pltpu.VMEM((width, rows), f32),
                pltpu.VMEM((width, slots), f32),
                pltpu.VMEM((width, rows), bf16),
                pltpu.VMEM((width, LANES), bf16),
                pltpu.VMEM((8, stages, CHUNKS, half, LANES), f32),
                pltpu.VMEM((8, stages, CHUNKS, half, LANES), f32),
                pltpu.VMEM((3, stages * CHUNKS, half, LANES), f32),
                pltpu.VMEM((ITERS, CHUNKS, links + 1, quarter, LANES), f32),
                pltpu.VMEM((links, 1, modes), jnp.int32),
                pltpu.VMEM((links, block, block), f32),
                dma((3,)),
                dma((8,)),
                dma((2, CHUNKS, 8)),
                dma((3,)),
                dma((3, 2, CHUNKS)),
                dma((links,)),
                dma((ITERS, CHUNKS)),
                dma((2, links)),
                dma((2, links)),
            ],
            compiler_params=pltpu.CompilerParams(
                collective_id=0, has_side_effects=True, vmem_limit_bytes=62 * 1024 * 1024
            ),
        )(source, schur, inverse, jnp.swapaxes(basis, 2, 3), coarse, pmap[:, :, None, :], counts, order)
        return pl.pallas_call(
            deliver,
            out_shape=(shape, shape),
            in_specs=[vmem, vmem],
            out_specs=(hbm, hbm),
            scratch_shapes=[dma((2,))],
            compiler_params=pltpu.CompilerParams(vmem_limit_bytes=1024 * 1024),
        )(*[pltpu.with_memory_space_constraint(value, pltpu.VMEM) for value in results])

    placed = (P("sx", "sy", None, None),) * 5 + (P("sx", "sy", None),) * 3
    return jax.shard_map(
        body,
        mesh=mesh,
        in_specs=placed,
        out_specs=(P("sx", "sy", None, None), P("sx", "sy", None, None)),
        check_vma=False,
    )
```
